32 devices in a mesh: pipe: 2 (over y), tensor: 4 (over z), dp: 4 (over x, core).
Axes of the slice: x: 2, y: 2, z: 4, core: 2. Of those that a mesh axis runs over, the one named last changes fastest.
Arguments:
- weights: bfloat16 [2, 4096, 4096], P('pipe', None, 'tensor'), may hold values from -0.09375 to 0.09375
- codes: int32 [2, 1024, 4096], P('pipe', 'dp'), may hold values from -127 to 127
- scales: float32 [2, 1024], P('pipe', 'dp'), may hold values from 0.004 to 0.04
- grad_out: bfloat16 [1024, 4096], P('dp', 'tensor'), may hold values from -6 to 6
Outputs:
- grad_in: bfloat16 [2, 1024, 4096], P('pipe', 'dp', 'tensor')
- weight_grad: float32 [2, 4096, 4096], P('pipe', 'dp', 'tensor')
The draws below stay inside these ranges and needn't reach their ends.
Inputs may be any that keep to these rules, and one draw needn't show every extreme that they name: Symmetric integer codes of a per-token quantization.
All inputs are finite; a program needn't handle non-finite values.
Results may differ from the reference program's by a relative error of at most 0.028.
Values may be sent and summed in bfloat16 or wider, within the bound.
A program may use at most 64 MiB of HBM per device.

```python
import math
import jax
import jax.numpy as jnp
from jax import lax

D = 4096
TOK_DEV = 256
TOKENS = 1024
SECTIONS = 2
COLS = 1024
N_TENSOR = 4
N_DP = 4


def with_ends(result, key, low, largest):
    extent = result.shape
    index_at = [jax.random.randint(jax.random.fold_in(key, axis), (), 0, extent[axis]) for axis in range(len(extent))]
    result = result.at[tuple(index_at)].set(low)
    longest = extent.index(max(extent))
    index_at[longest] = (index_at[longest] + 1) % extent[longest]
    return result.at[tuple(index_at)].set(largest)


def levels(own_key, dims, split, least, top_value):
    factor_of = 1.0
    for position, shards_of in split:
        steps = jax.random.uniform(jax.random.fold_in(jax.random.fold_in(own_key, 6), position), (shards_of,), jnp.float32, least / len(split), top_value / len(split))
        factor_of = factor_of * jnp.repeat(jnp.exp(steps), dims[position] // shards_of).reshape((-1,) + (1,) * (len(dims) - 1 - position))
    return factor_of


def centred(stream_key, shape, deviation, most, cuts=(), held_as=jnp.bfloat16):
    gain = levels(stream_key, shape, cuts, -0.22, 0.18) if cuts else 1.0
    drawn = jax.random.normal(stream_key, shape, jnp.float32) * deviation * gain
    return jnp.minimum(jnp.maximum(drawn, -most), most).astype(held_as)


def setup_inputs(seed: int = 0) -> dict:
    key_of = jax.random.split(jax.random.key(seed), 5)
    weights = centred(key_of[0], (SECTIONS, D, D), D ** -0.5, 0.09375, ((0, 2), (2, 4)))
    codes = with_ends(jax.random.randint(key_of[1], (SECTIONS, TOKENS, D), -127, 128), jax.random.fold_in(key_of[1], 1), -127, 127).astype(jnp.int32)
    scales = jnp.clip(jnp.exp(math.log(0.04) - 2.30258502 * jax.random.uniform(key_of[2], (SECTIONS, TOKENS), jnp.float32) ** levels(key_of[2], (SECTIONS, TOKENS), ((0, 2), (1, 4)), -0.2, 0.2)), 0.004, 0.04)
    grad_out = centred(key_of[3], (TOKENS, D), 1.0, 6.0, ((0, 4), (1, 4)))
    return dict(weights=weights, codes=codes, scales=scales, grad_out=grad_out)


def reference(weights, codes, scales, grad_out):
    arriving = grad_out
    grad_list = []
    weight_list = []
    for section_index in range(SECTIONS - 1, -1, -1):
        section_weight = weights[section_index]

        def add_block(running, block_index):
            grad_block = lax.dynamic_slice_in_dim(arriving, block_index * COLS, COLS, 1)
            weight_block = lax.dynamic_slice_in_dim(section_weight, block_index * COLS, COLS, 1)
            block_term = lax.dot_general(grad_block, weight_block, (((1,), (1,)), ((), ())), preferred_element_type=jnp.float32).astype(jnp.bfloat16)
            block_term = lax.optimization_barrier(block_term)
            return running + block_term.astype(jnp.float32), None

        summed, _ = lax.scan(add_block, arriving.astype(jnp.float32), jnp.arange(N_TENSOR, dtype=jnp.int32))
        fresh_grad = summed.astype(jnp.bfloat16)
        dequant = (codes[section_index].astype(jnp.float32) * scales[section_index][:, None]).astype(jnp.bfloat16)
        section_arriving = arriving

        def add_group(running, group_index):
            start = group_index * TOK_DEV
            x_group = lax.dynamic_slice_in_dim(dequant, start, TOK_DEV, 0)
            g_group = lax.dynamic_slice_in_dim(section_arriving, start, TOK_DEV, 0)
            group_term = lax.dot_general(x_group, g_group, (((0,), (0,)), ((), ())), preferred_element_type=jnp.float32).astype(jnp.bfloat16)
            group_term = lax.optimization_barrier(group_term)
            return running + group_term.astype(jnp.float32), None

        weight_term, _ = lax.scan(add_group, jnp.zeros((D, D), jnp.float32), jnp.arange(N_DP, dtype=jnp.int32))
        grad_list.insert(0, fresh_grad)
        weight_list.insert(0, weight_term)
        arriving = fresh_grad
    return jnp.stack(grad_list), jnp.stack(weight_list)
```

```python
import functools

import jax
import jax.numpy as jnp
from jax import lax
from jax.experimental import pallas as pl
from jax.experimental.pallas import tpu as pltpu
from jax.sharding import PartitionSpec as P

MICRO = 4
NT = (((1,), (1,)), ((), ()))


def relay_kernel(
    weights, codes, scales, grad_out,
    grad_in, g_all, x_all,
    w_buf, c_buf, x_buf, g_buf, prod, from_left, from_right,
    w_sem, c_sem, g_sem, hop_sem,
    right_send, right_recv, left_send, left_recv,
    g_send, g_recv, x_send, x_recv, g_own, x_own,
    *, sections, shards, replicas, micro,
):
    section, shard, replica = (lax.axis_index(n) for n in ("pipe", "tensor", "dp"))
    is_last = section == sections - 1
    tok, cols = g_buf.shape
    rows = tok // micro
    width = x_buf.shape[2]

    barrier = pltpu.get_barrier_semaphore()

    def greet(condition, target):
        @pl.when(condition)
        def _():
            pl.semaphore_signal(barrier, inc=1, device_id=target)

    def w_copy(j):
        part = pl.ds(pl.multiple_of(j * cols, cols), cols)
        return pltpu.make_async_copy(weights.at[part, :], w_buf.at[part, :], w_sem.at[j])

    def c_copy(o):
        peer = lax.rem(replica + o, replicas)
        part = pl.ds(pl.multiple_of(peer * width, width), width)
        return pltpu.make_async_copy(codes.at[:, part], c_buf.at[o], c_sem.at[o])

    def micro_rows(m):
        return pl.ds(pl.multiple_of(m * rows, rows), rows)

    def g_load(m):
        return pltpu.make_async_copy(grad_out.at[micro_rows(m), :], g_buf.at[micro_rows(m), :], g_sem.at[m])

    def order(i):
        return jnp.where(2 * shard < shards, shards - 1 - i, i)

    @pl.when(is_last)
    def _():
        @pl.loop(0, micro)
        def _(m):
            g_load(m).start()

    @pl.loop(0, shards)
    def _(i):
        w_copy(order(i)).start()

    @pl.loop(0, replicas)
    def _(o):
        c_copy(o).start()

    greet(shard > 0, {"tensor": shard - 1})
    greet(shard < shards - 1, {"tensor": shard + 1})
    greet(section > 0, {"pipe": section - 1})
    greet(section < sections - 1, {"pipe": section + 1})

    @pl.loop(1, replicas)
    def _(o):
        pl.semaphore_signal(barrier, inc=1, device_id={"dp": lax.rem(replica + o, replicas)})

    def one(condition):
        return jnp.where(condition, 1, 0)

    pl.semaphore_wait(
        barrier,
        replicas - 1 + one(shard > 0) + one(shard < shards - 1) + one(section > 0) + one(section < sections - 1),
    )

    def hop(m):
        return pltpu.make_async_remote_copy(
            src_ref=grad_in.at[micro_rows(m), :], dst_ref=g_buf.at[micro_rows(m), :],
            send_sem=hop_sem.at[m], recv_sem=g_sem.at[m], device_id={"pipe": section - 1})

    def to_right(m, j):
        return pltpu.make_async_remote_copy(
            src_ref=prod.at[m, j], dst_ref=from_left.at[m, j],
            send_sem=right_send.at[m, j], recv_sem=right_recv.at[m, j], device_id={"tensor": shard + 1})

    def to_left(m, j):
        return pltpu.make_async_remote_copy(
            src_ref=prod.at[m, j], dst_ref=from_right.at[m, j],
            send_sem=left_send.at[m, j], recv_sem=left_recv.at[m, j], device_id={"tensor": shard - 1})

    def own_rows(source):
        return pl.ds(pl.multiple_of(source * tok, tok), tok)

    def g_share(m, o):
        landing = pl.ds(pl.multiple_of(replica * tok + m * rows, rows), rows)
        return pltpu.make_async_remote_copy(
            src_ref=g_buf.at[micro_rows(m), :], dst_ref=g_all.at[landing, :],
            send_sem=g_send.at[m, o], recv_sem=g_recv.at[m, o],
            device_id={"dp": lax.rem(replica + o, replicas)})

    def g_keep(m):
        landing = pl.ds(pl.multiple_of(replica * tok + m * rows, rows), rows)
        return pltpu.make_async_copy(g_buf.at[micro_rows(m), :], g_all.at[landing, :], g_own.at[m])

    def x_share(o):
        return pltpu.make_async_remote_copy(
            src_ref=x_buf.at[o], dst_ref=x_all.at[own_rows(replica), :],
            send_sem=x_send.at[o], recv_sem=x_recv.at[o],
            device_id={"dp": lax.rem(replica + o, replicas)})

    def x_keep():
        return pltpu.make_async_copy(x_buf.at[0], x_all.at[own_rows(replica), :], x_own)

    def dequantize():
        @pl.loop(0, replicas)
        def _(i):
            o = replicas - 1 - i
            c_copy(o).wait()

            @pl.loop(0, micro)
            def _(m):
                part = micro_rows(m)
                value = c_buf[o, part, :].astype(jnp.float32) * scales[part, :]
                x_buf[o, part, :] = value.astype(jnp.bfloat16)

            @pl.when(o > 0)
            def _():
                x_share(o).start()

        x_keep().start()

    def produce(m):
        @pl.when(is_last)
        def _():
            g_load(m).wait()

        @pl.when(jnp.logical_not(is_last))
        def _():
            hop(m).wait_recv()

        @pl.loop(0, shards)
        def _(i):
            j = order(i)

            @pl.when(m == 0)
            def _():
                w_copy(j).wait()

            part = pl.ds(pl.multiple_of(j * cols, cols), cols)
            prod[m, j] = lax.dot_general(
                g_buf[micro_rows(m), :], w_buf[part, :], NT, preferred_element_type=jnp.float32
            ).astype(jnp.bfloat16)

            @pl.when((shard == 0) & (j > 0))
            def _():
                to_right(m, j).start()

            @pl.when((shard == shards - 1) & (j < shards - 1))
            def _():
                to_left(m, j).start()

        g_keep(m).start()

        @pl.loop(1, replicas)
        def _(o):
            g_share(m, o).start()

    def add_in(m, j, arrived):
        total = prod[m, j].astype(jnp.float32) + arrived[m, j].astype(jnp.float32)
        prod[m, j] = total.astype(jnp.bfloat16)

    def relay(m):
        @pl.loop(0, shards - 1)
        def _(i):
            far = shards - 1 - i

            @pl.when((shard > 0) & (shard + far < shards))
            def _():
                j = shard + far
                to_right(m, j).wait_recv()
                add_in(m, j, from_left)
                to_right(m, j).start()

            @pl.when((shard < shards - 1) & (shard - far >= 0))
            def _():
                j = shard - far
                to_left(m, j).wait_recv()
                add_in(m, j, from_right)
                to_left(m, j).start()

    def finish(m):
        part = micro_rows(m)

        @pl.when(shard > 0)
        def _():
            to_right(m, shard).wait_recv()

        @pl.when(shard < shards - 1)
        def _():
            to_left(m, shard).wait_recv()

        own = prod[m, shard].astype(jnp.float32) + g_buf[part, :].astype(jnp.float32)

        @pl.when((shard > 0) & (shard < shards - 1))
        def _():
            both = from_left[m, shard].astype(jnp.float32) + from_right[m, shard].astype(jnp.float32)
            grad_in[part, :] = (own + both).astype(jnp.bfloat16)

        @pl.when(shard == 0)
        def _():
            grad_in[part, :] = (own + from_right[m, shard].astype(jnp.float32)).astype(jnp.bfloat16)

        @pl.when(shard == shards - 1)
        def _():
            grad_in[part, :] = (own + from_left[m, shard].astype(jnp.float32)).astype(jnp.bfloat16)

        @pl.when(section > 0)
        def _():
            hop(m).start()

    @pl.when(jnp.logical_not(is_last))
    def _():
        dequantize()

    @pl.loop(0, micro + 1)
    def _(i):
        @pl.when(i < micro)
        def _():
            produce(i)

        @pl.when((i == 0) & is_last)
        def _():
            dequantize()

        @pl.when(i > 0)
        def _():
            finish(i - 1)

        @pl.when(i < micro)
        def _():
            relay(i)

    @pl.loop(0, micro)
    def _(m):
        @pl.loop(0, shards)
        def _(j):
            @pl.when((j > shard))
            def _():
                to_right(m, j).wait_send()

            @pl.when((j < shard))
            def _():
                to_left(m, j).wait_send()

        @pl.when(section > 0)
        def _():
            hop(m).wait_send()

        g_keep(m).wait()

        @pl.loop(1, replicas)
        def _(o):
            g_share(m, o).wait_send()
            g_share(m, o).wait_recv()

    x_keep().wait()

    @pl.loop(1, replicas)
    def _(o):
        x_share(o).wait_send()
        x_share(o).wait_recv()


def per_device(weights, codes, scales, grad_out):
    sections, shards, replicas = (lax.axis_size(n) for n in ("pipe", "tensor", "dp"))
    tok, cols = grad_out.shape
    depth = weights.shape[1]
    width = depth // replicas
    rows = tok // MICRO
    low = jnp.bfloat16
    dma = pltpu.SemaphoreType.DMA
    anywhere = pl.BlockSpec(memory_space=pl.ANY)
    inside = pl.BlockSpec(memory_space=pltpu.VMEM)
    grad_in, g_all, x_all = pl.pallas_call(
        functools.partial(relay_kernel, sections=sections, shards=shards, replicas=replicas, micro=MICRO),
        out_shape=(
            jax.ShapeDtypeStruct((tok, cols), low),
            jax.ShapeDtypeStruct((replicas * tok, cols), low),
            jax.ShapeDtypeStruct((replicas * tok, width), low),
        ),
        in_specs=[anywhere, anywhere, inside, anywhere],
        out_specs=(inside, anywhere, anywhere),
        scratch_shapes=[
            pltpu.VMEM((depth, cols), low),
            pltpu.VMEM((replicas, tok, width), jnp.int32),
            pltpu.VMEM((replicas, tok, width), low),
            pltpu.VMEM((tok, cols), low),
            pltpu.VMEM((MICRO, shards, rows, cols), low),
            pltpu.VMEM((MICRO, shards, rows, cols), low),
            pltpu.VMEM((MICRO, shards, rows, cols), low),
            dma((shards,)), dma((replicas,)), dma((MICRO,)), dma((MICRO,)),
            dma((MICRO, shards)), dma((MICRO, shards)), dma((MICRO, shards)), dma((MICRO, shards)),
            dma((MICRO, replicas)), dma((MICRO, replicas)), dma((replicas,)), dma((replicas,)),
            dma((MICRO,)), dma(()),
        ],
        compiler_params=pltpu.CompilerParams(collective_id=0, has_side_effects=True, vmem_limit_bytes=48 * 2**20),
    )(weights[0], codes[0], scales[0][:, None], grad_out)
    weight_grad = lax.dot_general(x_all, g_all, (((0,), (0,)), ((), ())), preferred_element_type=jnp.float32)
    return grad_in[None], weight_grad[None]


def solution(mesh):
    placed = (P("pipe", None, "tensor"), P("pipe", "dp", None), P("pipe", "dp"), P("dp", "tensor"))
    return jax.shard_map(
        per_device,
        mesh=mesh,
        in_specs=placed,
        out_specs=(P("pipe", "dp", "tensor"), P("pipe", "dp", "tensor")),
        check_vma=False,
    )
```

```python
import functools

import jax
import jax.numpy as jnp
from jax import lax
from jax.experimental import pallas as pl
from jax.experimental.pallas import tpu as pltpu
from jax.sharding import PartitionSpec as P

SIXTEENTHS = (4, 4, 4, 4)
STRIPS = 2
NT = (((1,), (1,)), ((), ()))


def relay_kernel(
    weights, codes, scales, grad_out,
    grad_in, g_all, x_all,
    w_buf, c_buf, s_buf, x_buf, g_buf, prod, from_left, from_right,
    w_sem, c_sem, g_sem, g_hop, hop_sem,
    right_send, right_recv, left_send, left_recv,
    g_send, g_recv, x_send, x_recv, g_own, x_own,
    *, sections, shards, replicas, pieces,
):
    section, shard, replica = (lax.axis_index(n) for n in ("pipe", "tensor", "dp"))
    is_last = section == sections - 1
    tok, cols = g_buf.shape
    micro = len(pieces)
    width = x_buf.shape[2]

    barrier = pltpu.get_barrier_semaphore()

    def greet(condition, target):
        @pl.when(condition)
        def _():
            pl.semaphore_signal(barrier, inc=1, device_id=target)

    def w_copy(j):
        part = pl.ds(pl.multiple_of(j * cols, cols), cols)
        return pltpu.make_async_copy(weights.at[part, :], w_buf.at[part, :], w_sem.at[j])

    def c_copy(o):
        peer = lax.rem(replica + o, replicas)
        part = pl.ds(pl.multiple_of(peer * width, width), width)
        return pltpu.make_async_copy(codes.at[:, part], c_buf.at[o], c_sem.at[o])

    def micro_rows(m):
        return pl.ds(*pieces[m])

    def head(ref, m, j):
        return ref.at[m, j, pl.ds(0, pieces[m][1]), :]

    def strip(m, h):
        size = pieces[m][1] // STRIPS
        return pl.ds(h * size, size)

    def strip_rows(m, h):
        size = pieces[m][1] // STRIPS
        return pl.ds(pieces[m][0] + h * size, size)

    def g_load(m):
        return pltpu.make_async_copy(grad_out.at[micro_rows(m), :], g_buf.at[micro_rows(m), :], g_sem.at[m])

    def order(i):
        return jnp.where(2 * shard < shards, shards - 1 - i, i)

    @pl.when(is_last)
    def _():
        for m in range(micro):
            g_load(m).start()

    @pl.loop(0, shards)
    def _(i):
        w_copy(order(i)).start()

    @pl.loop(0, replicas)
    def _(o):
        c_copy(o).start()

    greet(shard > 0, {"tensor": shard - 1})
    greet(shard < shards - 1, {"tensor": shard + 1})
    greet(section > 0, {"pipe": section - 1})
    greet(section < sections - 1, {"pipe": section + 1})

    @pl.loop(1, replicas)
    def _(o):
        pl.semaphore_signal(barrier, inc=1, device_id={"dp": lax.rem(replica + o, replicas)})

    def one(condition):
        return jnp.where(condition, 1, 0)

    pl.semaphore_wait(
        barrier,
        replicas - 1 + one(shard > 0) + one(shard < shards - 1) + one(section > 0) + one(section < sections - 1),
    )

    def hop(m, h):
        return pltpu.make_async_remote_copy(
            src_ref=grad_in.at[strip_rows(m, h), :], dst_ref=g_buf.at[strip_rows(m, h), :],
            send_sem=hop_sem.at[m * STRIPS + h], recv_sem=g_hop.at[m * STRIPS + h], device_id={"pipe": section - 1})

    def to_right(m, j, h):
        return pltpu.make_async_remote_copy(
            src_ref=prod.at[m, j, strip(m, h), :], dst_ref=from_left.at[m, j, strip(m, h), :],
            send_sem=right_send.at[m * STRIPS + h, j], recv_sem=right_recv.at[m * STRIPS + h, j], device_id={"tensor": shard + 1})

    def to_left(m, j, h):
        return pltpu.make_async_remote_copy(
            src_ref=prod.at[m, j, strip(m, h), :], dst_ref=from_right.at[m, j, strip(m, h), :],
            send_sem=left_send.at[m * STRIPS + h, j], recv_sem=left_recv.at[m * STRIPS + h, j], device_id={"tensor": shard - 1})

    def own_rows(source):
        return pl.ds(pl.multiple_of(source * tok, tok), tok)

    def g_share(m, o):
        landing = pl.ds(pl.multiple_of(replica * tok + pieces[m][0], 16), pieces[m][1])
        return pltpu.make_async_remote_copy(
            src_ref=g_buf.at[micro_rows(m), :], dst_ref=g_all.at[landing, :],
            send_sem=g_send.at[m, o], recv_sem=g_recv.at[m, o],
            device_id={"dp": lax.rem(replica + o, replicas)})

    def g_keep(m):
        landing = pl.ds(pl.multiple_of(replica * tok + pieces[m][0], 16), pieces[m][1])
        return pltpu.make_async_copy(g_buf.at[micro_rows(m), :], g_all.at[landing, :], g_own.at[m])

    def x_share(o):
        return pltpu.make_async_remote_copy(
            src_ref=x_buf.at[o], dst_ref=x_all.at[own_rows(replica), :],
            send_sem=x_send.at[o], recv_sem=x_recv.at[o],
            device_id={"dp": lax.rem(replica + o, replicas)})

    def x_keep():
        return pltpu.make_async_copy(x_buf.at[0], x_all.at[own_rows(replica), :], x_own)

    def dequantize():
        s_buf[...] = jnp.transpose(jnp.broadcast_to(scales[...], (128, tok)))

        @pl.loop(0, replicas)
        def _(i):
            o = replicas - 1 - i
            c_copy(o).wait()

            @pl.loop(0, 4)
            def _(m):
                part = pl.ds(pl.multiple_of(m * (tok // 4), tok // 4), tok // 4)
                value = c_buf[o, part, :].astype(jnp.float32) * s_buf[part, 0:1]
                x_buf[o, part, :] = value.astype(jnp.bfloat16)

            @pl.when(o > 0)
            def _():
                x_share(o).start()

        x_keep().start()

    def produce(m):
        @pl.when(is_last)
        def _():
            g_load(m).wait()

        @pl.when(jnp.logical_not(is_last))
        def _():
            for h in range(STRIPS):
                hop(m, h).wait_recv()

        @pl.loop(0, shards)
        def _(i):
            j = order(i)

            if m == 0:
                w_copy(j).wait()

            part = pl.ds(pl.multiple_of(j * cols, cols), cols)
            head(prod, m, j)[...] = lax.dot_general(
                g_buf[micro_rows(m), :], w_buf[part, :], NT, preferred_element_type=jnp.float32
            ).astype(jnp.bfloat16)

            @pl.when((shard == 0) & (j > 0))
            def _():
                for h in range(STRIPS):
                    to_right(m, j, h).start()

            @pl.when((shard == shards - 1) & (j < shards - 1))
            def _():
                for h in range(STRIPS):
                    to_left(m, j, h).start()

        g_keep(m).start()

        @pl.loop(1, replicas)
        def _(o):
            g_share(m, o).start()

    def add_in(m, j, h, arrived):
        part = strip(m, h)
        total = prod[m, j, part, :].astype(jnp.float32) + arrived[m, j, part, :].astype(jnp.float32)
        prod[m, j, part, :] = total.astype(jnp.bfloat16)

    def relay(m, rightward):
        @pl.loop(0, shards - 1)
        def _(i):
            far = shards - 1 - i

            @pl.when(rightward & (shard > 0) & (shard + far < shards))
            def _():
                j = shard + far
                for h in range(STRIPS):
                    to_right(m, j, h).wait_recv()
                    add_in(m, j, h, from_left)
                    to_right(m, j, h).start()

            @pl.when(jnp.logical_not(rightward) & (shard < shards - 1) & (shard - far >= 0))
            def _():
                j = shard - far
                for h in range(STRIPS):
                    to_left(m, j, h).wait_recv()
                    add_in(m, j, h, from_right)
                    to_left(m, j, h).start()

    def finish(m, h):
        part, inner = strip_rows(m, h), strip(m, h)

        @pl.when(shard > 0)
        def _():
            to_right(m, shard, h).wait_recv()

        @pl.when(shard < shards - 1)
        def _():
            to_left(m, shard, h).wait_recv()

        def of(ref):
            return ref[m, shard, inner, :].astype(jnp.float32)

        own = of(prod) + g_buf[part, :].astype(jnp.float32)

        @pl.when((shard > 0) & (shard < shards - 1))
        def _():
            grad_in[part, :] = (own + (of(from_left) + of(from_right))).astype(jnp.bfloat16)

        @pl.when(shard == 0)
        def _():
            grad_in[part, :] = (own + of(from_right)).astype(jnp.bfloat16)

        @pl.when(shard == shards - 1)
        def _():
            grad_in[part, :] = (own + of(from_left)).astype(jnp.bfloat16)

        @pl.when(section > 0)
        def _():
            hop(m, h).start()

    @pl.when(jnp.logical_not(is_last))
    def _():
        dequantize()

    near = 2 * shard < shards
    produce(0)

    @pl.when(is_last)
    def _():
        dequantize()

    for m in range(micro):
        relay(m, near)
        relay(m, jnp.logical_not(near))
        if m + 1 < micro:
            produce(m + 1)
        for h in range(STRIPS):
            finish(m, h)

    for m in range(micro):

        @pl.loop(0, shards)
        def _(j):
            @pl.when((j > shard))
            def _():
                for h in range(STRIPS):
                    to_right(m, j, h).wait_send()

            @pl.when((j < shard))
            def _():
                for h in range(STRIPS):
                    to_left(m, j, h).wait_send()

        @pl.when(section > 0)
        def _():
            for h in range(STRIPS):
                hop(m, h).wait_send()

        g_keep(m).wait()

        @pl.loop(1, replicas)
        def _(o):
            g_share(m, o).wait_send()
            g_share(m, o).wait_recv()

    x_keep().wait()

    @pl.loop(1, replicas)
    def _(o):
        x_share(o).wait_send()
        x_share(o).wait_recv()


def per_device(weights, codes, scales, grad_out):
    sections, shards, replicas = (lax.axis_size(n) for n in ("pipe", "tensor", "dp"))
    tok, cols = grad_out.shape
    depth = weights.shape[1]
    width = depth // replicas
    sizes = [tok * part // 16 for part in SIXTEENTHS]
    pieces = tuple((sum(sizes[:m]), size) for m, size in enumerate(sizes))
    micro, rows = len(sizes), max(sizes)
    strips = micro * STRIPS
    low = jnp.bfloat16
    dma = pltpu.SemaphoreType.DMA
    anywhere = pl.BlockSpec(memory_space=pl.ANY)
    far = pl.BlockSpec(memory_space=pltpu.MemorySpace.HBM)
    inside = pl.BlockSpec(memory_space=pltpu.VMEM)
    grad_in, g_all, x_all = pl.pallas_call(
        functools.partial(relay_kernel, sections=sections, shards=shards, replicas=replicas, pieces=pieces),
        out_shape=(
            jax.ShapeDtypeStruct((tok, cols), low),
            jax.ShapeDtypeStruct((replicas * tok, cols), low),
            jax.ShapeDtypeStruct((replicas * tok, width), low),
        ),
        in_specs=[far, far, inside, far],
        out_specs=(inside, anywhere, anywhere),
        scratch_shapes=[
            pltpu.VMEM((depth, cols), low),
            pltpu.VMEM((replicas, tok, width), jnp.int32),
            pltpu.VMEM((tok, 128), jnp.float32),
            pltpu.VMEM((replicas, tok, width), low),
            pltpu.VMEM((tok, cols), low),
            pltpu.VMEM((micro, shards, rows, cols), low),
            pltpu.VMEM((micro, shards, rows, cols), low),
            pltpu.VMEM((micro, shards, rows, cols), low),
            dma((shards,)), dma((replicas,)), dma((micro,)), dma((strips,)), dma((strips,)),
            dma((strips, shards)), dma((strips, shards)), dma((strips, shards)), dma((strips, shards)),
            dma((micro, replicas)), dma((micro, replicas)), dma((replicas,)), dma((replicas,)),
            dma((micro,)), dma(()),
        ],
        compiler_params=pltpu.CompilerParams(collective_id=0, has_side_effects=True, vmem_limit_bytes=48 * 2**20),
    )(weights[0], codes[0], scales, grad_out)
    weight_grad = lax.dot_general(x_all, g_all, (((0,), (0,)), ((), ())), preferred_element_type=jnp.float32)
    return grad_in[None], weight_grad[None]


def solution(mesh):
    placed = (P("pipe", None, "tensor"), P("pipe", "dp", None), P("pipe", "dp"), P("dp", "tensor"))
    return jax.shard_map(
        per_device,
        mesh=mesh,
        in_specs=placed,
        out_specs=(P("pipe", "dp", "tensor"), P("pipe", "dp", "tensor")),
        check_vma=False,
    )
```
